32 devices in a mesh: layer: 2 (over y), latent: 8 (over z, x), tok: 2 (over core).
Axes of the slice: x: 2, y: 2, z: 4, core: 2. Of those that a mesh axis runs over, the one named last changes fastest.
Arguments:
- resid: bfloat16 [2, 384, 2304], P('layer', 'tok', 'latent'), may hold values from -6 to 6
- w_enc: bfloat16 [2, 2304, 2048], P('layer', None, 'latent'), may hold values from -0.09375 to 0.09375
- b_enc: float32 [2048], P('latent'), may hold values from -3 to 3
- w_dec: bfloat16 [2, 2048, 2304], P('layer', 'latent'), may hold values from -0.125 to 0.125
- b_dec: bfloat16 [2, 2304], P('layer', 'latent'), may hold values from -3 to 3
Outputs:
- grad_w_enc: bfloat16 [2, 2304, 2048], P('layer', 'tok', 'latent')
- grad_w_dec: bfloat16 [2, 2048, 2304], P('layer', 'latent')
The draws below stay inside these ranges and needn't reach their ends.
All inputs are finite; a program needn't handle non-finite values.
Results may differ from the reference program's by a relative error of at most 0.023.
Values may be sent and summed in bfloat16 or wider, within the bound.
A program may use at most 64 MiB of HBM per device.

```python
import jax
import jax.numpy as jnp
from jax import lax

D = 2304
H_DEV = 256
TOK_DEV = 192
H = 2048
LAYERS = 2
TOKENS = 384
N_LATENT = 8
N_TOK = 2


def block_levels(rng, dims, shards, least, high):
    factor_of, own = 1.0, jax.random.fold_in(rng, 6)
    for axis_at, blocks in shards:
        steps = jnp.exp(jax.random.uniform(jax.random.fold_in(own, axis_at), (blocks,), jnp.float32, least / len(shards), high / len(shards)))
        factor_of = factor_of * jnp.repeat(steps, dims[axis_at] // blocks).reshape([-1 if axis == axis_at else 1 for axis in range(len(dims))])
    return factor_of


def noise(stream_key, extent, deviation, reach, cuts=(), dtype=jnp.bfloat16):
    drawn = deviation * jax.random.normal(stream_key, extent, jnp.float32)
    if cuts:
        drawn = drawn * block_levels(stream_key, extent, cuts, -0.22, 0.18)
    return jnp.clip(drawn, -reach, reach).astype(dtype)


def setup_inputs(seed: int = 0) -> dict:
    key_list = jax.random.split(jax.random.key(seed), 6)
    return {
        "resid": noise(key_list[0], (LAYERS, TOKENS, D), 1.0, 6.0, ((0, 2), (1, 2), (2, 8))),
        "w_enc": noise(key_list[1], (LAYERS, D, H), (D * LAYERS) ** -0.5, 0.09375, ((0, 2), (2, 8))),
        "b_enc": noise(key_list[2], (H,), 0.5, 3.0, ((0, 8),), jnp.float32),
        "w_dec": noise(key_list[3], (LAYERS, H, D), H ** -0.5, 0.125, ((0, 2), (1, 8))),
        "b_dec": noise(key_list[4], (LAYERS, D), 0.5, 3.0, ((0, 2), (1, 8))),
    }


BETA = 4.0


def halves(left, right):
    total = jnp.zeros((left.shape[1], right.shape[1]), jnp.float32)
    for block in range(N_TOK):
        lo = block * TOK_DEV
        part = jnp.dot(left[lo:lo + TOK_DEV].T, right[lo:lo + TOK_DEV], preferred_element_type=jnp.float32)
        part = lax.optimization_barrier(part.astype(jnp.bfloat16)).astype(jnp.float32)
        total = total + part
    return total.astype(jnp.bfloat16)


def slab_sum(act, layer_w):
    act_slabs = jnp.transpose(act.reshape(TOKENS, N_LATENT, H_DEV), (1, 0, 2))
    w_slabs = layer_w.reshape(N_LATENT, H_DEV, D)

    def add_slab(carry, items):
        act_slab, w_slab = items
        part = jnp.dot(act_slab, w_slab, preferred_element_type=jnp.float32)
        part = lax.optimization_barrier(part.astype(jnp.bfloat16)).astype(jnp.float32)
        return carry + part, None

    total, _ = lax.scan(add_slab, jnp.zeros((TOKENS, D), jnp.float32), (act_slabs, w_slabs))
    return total


def reference(resid, w_enc, b_enc, w_dec, b_dec):
    def encode(carry, items):
        layer_x, layer_w = items
        return carry + jnp.dot(layer_x, layer_w, preferred_element_type=jnp.float32), None

    start = jnp.broadcast_to(b_enc.astype(jnp.float32), (TOKENS, H))
    pre, _ = lax.scan(encode, start, (resid, w_enc))
    act = (jax.nn.softplus(BETA * pre) / BETA).astype(jnp.bfloat16)
    slope = jax.nn.sigmoid(BETA * pre)

    def decode(carry, items):
        layer_x, layer_w, layer_b = items
        recon = slab_sum(act, layer_w) + layer_b.astype(jnp.float32)
        grad_recon = ((2.0 / TOKENS) * (recon - layer_x.astype(jnp.float32))).astype(jnp.bfloat16)
        carry = carry + jnp.dot(grad_recon, layer_w.T, preferred_element_type=jnp.float32)
        return carry, halves(act, grad_recon)

    grad_act, grad_w_dec = lax.scan(decode, jnp.zeros((TOKENS, H), jnp.float32), (resid, w_dec, b_dec))
    grad_pre = (grad_act * slope).astype(jnp.bfloat16)
    grad_w_enc = lax.map(lambda layer_x: halves(layer_x, grad_pre), resid)
    return grad_w_enc, grad_w_dec
```

```python
import functools

import jax
import jax.numpy as jnp
from jax import lax
from jax.experimental import pallas as pl
from jax.experimental.pallas import tpu as pltpu
from jax.sharding import PartitionSpec as P

BETA = 4.0
LANES = 128
CHUNKS = 3
MESH = pl.DeviceIdType.MESH
F32 = jnp.float32
BF16 = jnp.bfloat16


def plain_shards(resid, w_enc, b_enc, w_dec, b_dec):
    decoder = w_dec[0]
    x_full = lax.all_gather(resid, "latent", axis=2, tiled=True)[0]
    bias_full = lax.all_gather(b_dec.reshape(1, 1, -1), "latent", axis=2, tiled=True)
    bias_full = bias_full.reshape(-1).astype(F32)
    tokens = x_full.shape[0] * lax.axis_size("tok")
    partial_value = jnp.dot(x_full, w_enc[0], preferred_element_type=F32)
    pre = lax.psum(partial_value.astype(BF16), "layer").astype(F32) + b_enc
    act = (jax.nn.softplus(BETA * pre) / BETA).astype(BF16)
    slope = jax.nn.sigmoid(BETA * pre)
    recon = lax.psum(
        jnp.dot(act, decoder, preferred_element_type=F32).astype(BF16), "latent"
    ).astype(F32)
    grad_all = (2.0 / tokens * (recon + bias_full - x_full.astype(F32))).astype(BF16)
    dec_sum = lax.dot_general(
        act, grad_all, (((0,), (0,)), ((), ())), preferred_element_type=F32
    )
    act_grad = lax.dot_general(
        grad_all, decoder, (((1,), (1,)), ((), ())), preferred_element_type=F32
    )
    grad_act = lax.psum(act_grad.astype(BF16), "layer").astype(F32)
    grad_pre = (grad_act * slope).astype(BF16)
    grad_w_dec = lax.psum(dec_sum.astype(BF16), "tok")
    grad_w_enc = lax.psum_scatter(
        lax.dot_general(
            x_full, grad_pre, (((0,), (0,)), ((), ())), preferred_element_type=F32
        ).astype(BF16),
        "tok",
        scatter_dimension=0,
        tiled=True,
    )
    return (grad_w_enc[None], grad_w_dec[None])


def kernel(
    n_lat, tokens,
    x_hbm, we_hbm, be_hbm, wd_hbm, bd_hbm,
    oe_ref, od_ref,
    x_ref, be_ref, bd_ref, we, wdv, wd, xb, xo, xt, gb, go, pre, slope, act, act_t, act_o, ys, yr, hs, hr, gp, gp_o,
    xs, xr, zs, cr, bias_x,
    load_sem, we_sem, x_ss, x_rs, xo_ss, xo_rs, g_ss, g_rs, go_ss, go_rs, one_ss, one_rs, xs_ss, xr_rs, zs_ss, cr_rs,
):
    rows, feats = x_ref.shape
    hid = we.shape[2]
    main = feats // LANES * LANES
    tiles = main // LANES
    rest = feats - main
    groups = LANES // rest
    part = rows // CHUNKS
    sub = part // groups
    nz = n_lat // 2
    half = n_lat // 2

    lay = lax.axis_index("layer")
    lat = lax.axis_index("latent")
    tok = lax.axis_index("tok")
    z, xx = lat // 2, lat % 2
    across = {"latent": 2 * z + 1 - xx}
    other_layer = {"layer": 1 - lay}
    tok_o = 1 - tok
    other_tok = {"tok": tok_o}
    inner = jnp.logical_and(z > 0, z < nz - 1)

    def peer(k):
        if k == 0:
            return z
        if k == 1:
            return z + 1 - 2 * (z % 2)
        if k == 2:
            return (z + 2) % 4
        return nz - 1 - z

    def same(k):
        return 2 * peer(k) + xx

    def cross(k):
        return 2 * peer(k) + 1 - xx

    loads = [
        pltpu.make_async_copy(src, dst, load_sem.at[i])
        for i, (src, dst) in enumerate(
            [(x_hbm, x_ref), (wd_hbm, wdv), (be_hbm, be_ref), (bd_hbm, bd_ref)]
        )
    ]
    we_loads = []
    for j in range(n_lat):
        lo = j * feats
        we_loads.append(pltpu.make_async_copy(
            we_hbm.at[pl.ds(lo, main)], we.at[j, pl.ds(0, main)], we_sem.at[j, 0]
        ))
        for g in range(groups):
            we_loads.append(pltpu.make_async_copy(
                we_hbm.at[pl.ds(lo + main, rest)], we.at[j, pl.ds(main + g * rest, rest)],
                we_sem.at[j, 1 + g],
            ))
    loads[0].start()
    x_load, wd_load, be_load, bd_load = loads

    barrier = pltpu.get_barrier_semaphore()

    def greet(where):
        pl.semaphore_signal(barrier, inc=1, device_id=where, device_id_type=MESH)

    for k in range(1, nz):
        greet({"latent": same(k)})
    greet(across)
    greet(other_layer)
    greet(other_tok)
    for load in loads[1:] + we_loads:
        load.start()

    def remote(src, dst, ss, rs, where):
        return pltpu.make_async_remote_copy(
            src_ref=src, dst_ref=dst, send_sem=ss, recv_sem=rs,
            device_id=where, device_id_type=MESH,
        )

    lane = lax.broadcasted_iota(jnp.int32, (sub, LANES), 1) // rest

    def pack(full):
        out = jnp.zeros((sub, LANES), F32)
        for g in range(groups):
            out = jnp.where(lane == g, full[g * sub:(g + 1) * sub, main:], out)
        return jnp.concatenate(
            [full[:, i * LANES:(i + 1) * LANES] for i in range(tiles)] + [out], axis=0
        )

    def spread(block):
        packed = block[tiles * part:]
        zero = jnp.zeros_like(packed)
        parts = jnp.concatenate(
            [jnp.where(lane == g, packed, zero) for g in range(groups)], axis=0
        )
        return jnp.concatenate(
            [block[i * part:(i + 1) * part] for i in range(tiles)] + [parts], axis=1
        )

    def spread_all(ref, j):
        return [spread(ref[c, j]) for c in range(CHUNKS)]

    def gather(buf, ss, rs):
        def send(way, c, j):
            where = across if way == 0 else {"latent": same(way)}
            return remote(buf.at[c, j], buf.at[c, j], ss.at[way, c, j], rs.at[c, j], where)

        def own(c):
            send(0, c, lat).start()
            send(1, c, lat).start()
            pl.when(inner)(lambda: send(3, c, lat).start())
            send(2, c, lat).start()

        def relay(c, k):
            j = same(k)
            send(0, c, j).wait_recv()
            send(0, c, j).start()
            if k == 2:
                pl.when(inner)(lambda: send(1, c, j).start())

        def arrive(c, k):
            send(0, c, cross(k)).wait_recv()

        def finish():
            for c in range(CHUNKS):
                for k in range(nz):
                    send(0, c, same(k)).wait_send()
                send(1, c, lat).wait_send()
                send(2, c, lat).wait_send()

                @pl.when(inner)
                def _():
                    send(3, c, lat).wait_send()
                    send(1, c, same(2)).wait_send()

        return own, relay, arrive, finish

    x_own, x_relay, x_arrive, x_finish = gather(xb, x_ss, x_rs)
    g_own, g_relay, g_arrive, g_finish = gather(gb, g_ss, g_rs)

    def x_tok(i):
        return remote(
            xb.at[:, half * tok_o + i], xo.at[:, i], xo_ss.at[i], xo_rs.at[i], other_tok
        )

    def g_tok(c):
        return remote(gb.at[c], go.at[c], go_ss.at[c], go_rs.at[c], other_tok)

    def one(i, src, dst, c, where):
        return remote(src.at[c], dst.at[c], one_ss.at[i, c], one_rs.at[i, c], where)

    def y_copy(c):
        return one(0, ys, yr, c, other_layer)

    def a_copy(c):
        return one(1, act, act_o, c, other_tok)

    def h_copy(c):
        return one(2, hs, hr, c, other_layer)

    def p_copy(c):
        return one(3, gp, gp_o, c, other_tok)

    def x_send(c, k):
        return remote(xs.at[c, k], xr.at[c, k], xs_ss.at[c, k], xr_rs.at[c, k], across)

    def z_send(c, k):
        return remote(
            zs.at[c, k], cr.at[c, k], zs_ss.at[c, k], cr_rs.at[c, k], {"latent": same(k)}
        )

    def encode(c, j):
        pre[c] += jnp.dot(spread(xb[c, j]), we[j], preferred_element_type=F32)

    def y_out(c):
        ys[c] = pre[c].astype(BF16)
        y_copy(c).start()

    def activate(c):
        y_copy(c).wait_recv()
        v = BETA * (pre[c] + yr[c].astype(F32) + be_ref[...])
        e = jnp.exp(-jnp.abs(v))
        act[c] = ((jnp.maximum(v, 0.0) + jnp.log1p(e)) / BETA).astype(BF16)
        slope[c] = jnp.where(v >= 0, 1.0, e) / (1.0 + e)
        a_copy(c).start()

    def decode(c, j):
        return pack(jnp.dot(act[c], wd[j], preferred_element_type=F32))

    def x_out(c, k):
        xs[c, k] = decode(c, cross(k)).astype(BF16)
        x_send(c, k).start()

    def z_out(c, k):
        mine = decode(c, same(k))
        x_send(c, k).wait_recv()
        zs[c, k] = (mine + xr[c, k].astype(F32)).astype(BF16)
        z_send(c, k).start()

    def settle(c):
        total = decode(c, lat) + bias_x[c]
        x_send(c, 0).wait_recv()
        total += xr[c, 0].astype(F32)
        for k in range(1, nz):
            z_send(c, k).wait_recv()
            total += cr[c, k].astype(F32)
        gb[c, lat] = (2.0 / tokens * total).astype(BF16)
        g_own(c)

    def back(c, j):
        d = lax.dot_general(
            spread(gb[c, j]), wd[j], (((1,), (1,)), ((), ())), preferred_element_type=F32
        )
        pre[c] += d

    def back_first(c):
        pre[c] = lax.dot_general(
            spread(gb[c, lat]), wd[lat], (((1,), (1,)), ((), ())), preferred_element_type=F32
        )

    def h_out(c):
        hs[c] = pre[c].astype(BF16)
        h_copy(c).start()
        g_tok(c).start()

    def grad_pre(c):
        h_copy(c).wait_recv()
        gp[c] = ((pre[c] + hr[c].astype(F32)) * slope[c]).astype(BF16)
        p_copy(c).start()

    def both(own, other, j_own, j_other):
        return jnp.concatenate(spread_all(own, j_own) + spread_all(other, j_other), axis=0)

    def turn_x():
        for i in range(half):
            x_tok(i).wait_recv()
            xt[i] = both(xb, xo, half * tok + i, i).T

    def turn_act():
        for c in range(CHUNKS):
            a_copy(c).wait_recv()
        act_t[...] = jnp.concatenate(
            [act[c] for c in range(CHUNKS)] + [act_o[c] for c in range(CHUNKS)], axis=0
        ).T

    def widen_decoder():
        wd_load.wait()
        for k in range(n_lat):
            lo = k * feats
            w_rest = wdv[:, lo + main:lo + feats]
            wd[k] = jnp.concatenate([wdv[:, lo:lo + main]] + [w_rest] * groups, axis=1)

    def fill_bias():
        bias = bd_ref[...].astype(F32)
        bias = jnp.concatenate([bias[:, :main]] + [bias[:, main:]] * groups, axis=1)
        block = jnp.concatenate(
            [jnp.broadcast_to(bias[:, i * LANES:(i + 1) * LANES], (part, LANES)) for i in range(tiles)]
            + [jnp.broadcast_to(bias[:, main:], (sub, LANES))],
            axis=0,
        )
        for c in range(CHUNKS):
            bias_x[c] = block - xb[c, lat].astype(F32)

    x_load.wait()
    tail = x_ref[:, main:]
    wide = jnp.concatenate([x_ref[:, :main]] + [tail] * groups, axis=1).astype(F32)
    for c in range(CHUNKS):
        xb[c, lat] = pack(wide[c * part:(c + 1) * part]).astype(BF16)

    pl.semaphore_wait(barrier, nz + 2)
    for c in range(CHUNKS):
        x_own(c)
    for load in we_loads:
        load.wait()
    be_load.wait()
    bd_load.wait()
    for c in range(CHUNKS):
        pre[c] = jnp.dot(spread(xb[c, lat]), we[lat], preferred_element_type=F32)
    widen_decoder()
    fill_bias()

    def relay_encode(c):
        for k in range(1, nz):
            x_relay(c, k)
        for k in range(1, nz):
            encode(c, same(k))

    def arrive_encode(c):
        for k in range(nz):
            x_arrive(c, k)
            encode(c, cross(k))

    relay_encode(0)
    relay_encode(1)
    arrive_encode(0)
    y_out(0)
    relay_encode(2)
    arrive_encode(1)
    y_out(1)
    activate(0)
    for k in (3, 2, 1, 0):
        x_out(0, k)
    arrive_encode(2)
    y_out(2)
    for i in range(half):
        x_tok(i).start()
    activate(1)
    for k in (3, 2, 1, 0):
        x_out(1, k)
    for k in (3, 2, 1):
        z_out(0, k)
    activate(2)
    for k in (3, 2, 1, 0):
        x_out(2, k)
    for k in (3, 2, 1):
        z_out(1, k)
    turn_x()
    settle(0)
    for k in (3, 2, 1):
        z_out(2, k)
    turn_act()
    settle(1)
    back_first(0)

    def relay_back(c):
        for k in range(1, nz):
            g_relay(c, k)
        for k in range(1, nz):
            back(c, same(k))

    def arrive_back(c):
        for k in range(nz):
            g_arrive(c, k)
            back(c, cross(k))

    relay_back(0)
    settle(2)
    back_first(1)
    back_first(2)
    relay_back(1)
    arrive_back(0)
    h_out(0)
    relay_back(2)
    arrive_back(1)
    h_out(1)
    grad_pre(0)
    arrive_back(2)
    h_out(2)
    grad_pre(1)
    for c in range(CHUNKS):
        g_tok(c).wait_recv()

    row = []
    for j in range(n_lat):
        dw = jnp.dot(act_t[...], both(gb, go, j, j), preferred_element_type=F32)
        r = dw[:, main:main + rest]
        for g in range(1, groups):
            r = r + dw[:, main + g * rest:main + (g + 1) * rest]
        row += [dw[:, :main], r]
        if (j + 1) * feats % LANES == 0:
            width = sum(p.shape[1] for p in row)
            od_ref[:, (j + 1) * feats - width:(j + 1) * feats] = jnp.concatenate(
                row, axis=1
            ).astype(BF16)
            row = []

    grad_pre(2)
    for c in range(CHUNKS):
        p_copy(c).wait_recv()
    gp_both = jnp.concatenate(
        [gp[c] for c in range(CHUNKS)] + [gp_o[c] for c in range(CHUNKS)], axis=0
    )
    for i in range(half):
        dw = jnp.dot(xt[i], gp_both, preferred_element_type=F32)
        r = dw[main:main + rest]
        for g in range(1, groups):
            r = r + dw[main + g * rest:main + (g + 1) * rest]
        oe_ref[i * feats:(i + 1) * feats] = jnp.concatenate([dw[:main], r], axis=0).astype(BF16)

    x_finish()
    g_finish()
    for i in range(half):
        x_tok(i).wait_send()
    for c in range(CHUNKS):
        for copy in (g_tok, y_copy, a_copy, h_copy, p_copy):
            copy(c).wait_send()
        x_send(c, 0).wait_send()
        for k in range(1, nz):
            x_send(c, k).wait_send()
            z_send(c, k).wait_send()


def fused_shards(n_lat, resid, w_enc, b_enc, w_dec, b_dec):
    x, we, wd = resid[0], w_enc[0], w_dec[0]
    rows, feats = x.shape
    total, hid = we.shape
    main = feats // LANES * LANES
    wide = main + LANES
    groups = LANES // (feats - main)
    part = rows // CHUNKS
    block = part * feats // LANES
    half, nz = n_lat // 2, n_lat // 2
    dma = pltpu.SemaphoreType.DMA
    vm = pltpu.VMEM
    blocks = vm((CHUNKS, n_lat, block, LANES), BF16)
    blocks_z = vm((CHUNKS, nz, block, LANES), BF16)
    square = vm((CHUNKS, part, hid), BF16)
    square_f = vm((CHUNKS, part, hid), F32)
    in_vmem = pl.BlockSpec(memory_space=pltpu.VMEM)
    in_hbm = pl.BlockSpec(memory_space=pltpu.HBM)
    ge, gd = pl.pallas_call(
        functools.partial(kernel, n_lat, rows * 2),
        out_shape=(
            jax.ShapeDtypeStruct((half * feats, hid), BF16),
            jax.ShapeDtypeStruct((hid, total), BF16),
        ),
        in_specs=[in_hbm] * 5,
        out_specs=(in_vmem, in_vmem),
        scratch_shapes=[
            vm((rows, feats), BF16), vm((1, hid), F32), vm((1, feats), BF16),
            vm((n_lat, wide, hid), BF16),
            vm((hid, total), BF16),
            vm((n_lat, hid, wide), BF16),
            blocks,
            vm((CHUNKS, half, block, LANES), BF16),
            vm((half, wide, 2 * rows), BF16),
            blocks, blocks,
            square_f, square_f,
            square, vm((hid, 2 * rows), BF16), square,
            square, square, square, square, square, square,
            blocks_z, blocks_z, blocks_z, blocks_z,
            vm((CHUNKS, block, LANES), F32),
            dma((4,)), dma((n_lat, 1 + groups)),
            dma((4, CHUNKS, n_lat)), dma((CHUNKS, n_lat)), dma((half,)), dma((half,)),
            dma((4, CHUNKS, n_lat)), dma((CHUNKS, n_lat)), dma((CHUNKS,)), dma((CHUNKS,)),
            dma((4, CHUNKS)), dma((4, CHUNKS)),
            dma((CHUNKS, nz)), dma((CHUNKS, nz)), dma((CHUNKS, nz)), dma((CHUNKS, nz)),
        ],
        compiler_params=pltpu.CompilerParams(
            collective_id=0, has_side_effects=True, vmem_limit_bytes=48 * 2**20
        ),
    )(*(
        pltpu.with_memory_space_constraint(v, pltpu.HBM)
        for v in (x, we, b_enc.reshape(1, -1), wd, b_dec)
    ))
    return ge[None], gd[None]


def packs(mesh, rows, feats):
    rest = feats % LANES
    if mesh.shape["layer"] != 2 or mesh.shape["tok"] != 2 or mesh.shape["latent"] != 8:
        return False
    if rest == 0 or rest % 32 or LANES % rest:
        return False
    return rows % (16 * CHUNKS * (LANES // rest)) == 0 and feats > LANES


def solution(mesh):
    def shards(resid, w_enc, b_enc, w_dec, b_dec):
        _, rows, feats = resid.shape
        if packs(mesh, rows, feats) and resid.shape[0] == 1:
            return fused_shards(mesh.shape["latent"], resid, w_enc, b_enc, w_dec, b_dec)
        return plain_shards(resid, w_enc, b_enc, w_dec, b_dec)

    placed = (
        P("layer", "tok", "latent"),
        P("layer", None, "latent"),
        P("latent"),
        P("layer", "latent", None),
        P("layer", "latent"),
    )
    return jax.shard_map(
        shards,
        mesh=mesh,
        in_specs=placed,
        out_specs=(P("layer", "tok", "latent"), P("layer", "latent", None)),
        check_vma=False,
    )
```

```python
import functools

import jax
import jax.numpy as jnp
from jax import lax
from jax.experimental import pallas as pl
from jax.experimental.pallas import tpu as pltpu
from jax.sharding import PartitionSpec as P

BETA = 4.0
LANES = 128
CHUNKS = 3
MESH = pl.DeviceIdType.MESH
F32 = jnp.float32
BF16 = jnp.bfloat16


def plain_shards(resid, w_enc, b_enc, w_dec, b_dec):
    decoder = w_dec[0]
    x_full = lax.all_gather(resid, "latent", axis=2, tiled=True)[0]
    bias_full = lax.all_gather(b_dec.reshape(1, 1, -1), "latent", axis=2, tiled=True)
    bias_full = bias_full.reshape(-1).astype(F32)
    tokens = x_full.shape[0] * lax.axis_size("tok")
    partial_value = jnp.dot(x_full, w_enc[0], preferred_element_type=F32)
    pre = lax.psum(partial_value.astype(BF16), "layer").astype(F32) + b_enc
    act = (jax.nn.softplus(BETA * pre) / BETA).astype(BF16)
    slope = jax.nn.sigmoid(BETA * pre)
    recon = lax.psum(
        jnp.dot(act, decoder, preferred_element_type=F32).astype(BF16), "latent"
    ).astype(F32)
    grad_all = (2.0 / tokens * (recon + bias_full - x_full.astype(F32))).astype(BF16)
    dec_sum = lax.dot_general(
        act, grad_all, (((0,), (0,)), ((), ())), preferred_element_type=F32
    )
    act_grad = lax.dot_general(
        grad_all, decoder, (((1,), (1,)), ((), ())), preferred_element_type=F32
    )
    grad_act = lax.psum(act_grad.astype(BF16), "layer").astype(F32)
    grad_pre = (grad_act * slope).astype(BF16)
    grad_w_dec = lax.psum(dec_sum.astype(BF16), "tok")
    grad_w_enc = lax.psum_scatter(
        lax.dot_general(
            x_full, grad_pre, (((0,), (0,)), ((), ())), preferred_element_type=F32
        ).astype(BF16),
        "tok",
        scatter_dimension=0,
        tiled=True,
    )
    return (grad_w_enc[None], grad_w_dec[None])


def kernel(
    n_lat, tokens,
    x_hbm, we_hbm, be_hbm, wd_hbm, bd_hbm,
    gp_both, xt, od_ref,
    x_ref, be_ref, bd_ref, we, wdv, wd, xb, xo, gb, go, pre, slope, act, act_t, act_o, ys, yr, hs, hr, gp, gp_o,
    xs, xr, zs, cr, bias_x,
    load_sem, we_sem, x_ss, x_rs, xo_ss, xo_rs, g_ss, g_rs, go_ss, go_rs, one_ss, one_rs, xs_ss, xr_rs, zs_ss, cr_rs,
):
    rows, feats = x_ref.shape
    hid = we.shape[2]
    main = feats // LANES * LANES
    tiles = main // LANES
    rest = feats - main
    groups = LANES // rest
    part = rows // CHUNKS
    sub = part // groups
    nz = n_lat // 2
    half = n_lat // 2

    lay = lax.axis_index("layer")
    lat = lax.axis_index("latent")
    tok = lax.axis_index("tok")
    z, xx = lat // 2, lat % 2
    across = {"latent": 2 * z + 1 - xx}
    other_layer = {"layer": 1 - lay}
    tok_o = 1 - tok
    other_tok = {"tok": tok_o}
    inner = jnp.logical_and(z > 0, z < nz - 1)

    def peer(k):
        if k == 0:
            return z
        if k == 1:
            return z + 1 - 2 * (z % 2)
        if k == 2:
            return (z + 2) % 4
        return nz - 1 - z

    def same(k):
        return 2 * peer(k) + xx

    def cross(k):
        return 2 * peer(k) + 1 - xx

    loads = [
        pltpu.make_async_copy(src, dst, load_sem.at[i])
        for i, (src, dst) in enumerate(
            [(x_hbm, x_ref), (wd_hbm, wdv), (be_hbm, be_ref), (bd_hbm, bd_ref)]
        )
    ]
    we_loads = []
    for j in range(n_lat):
        lo = j * feats
        we_loads.append(pltpu.make_async_copy(
            we_hbm.at[pl.ds(lo, main)], we.at[j, pl.ds(0, main)], we_sem.at[j, 0]
        ))
        for g in range(groups):
            we_loads.append(pltpu.make_async_copy(
                we_hbm.at[pl.ds(lo + main, rest)], we.at[j, pl.ds(main + g * rest, rest)],
                we_sem.at[j, 1 + g],
            ))
    loads[0].start()
    x_load, wd_load, be_load, bd_load = loads

    barrier = pltpu.get_barrier_semaphore()

    def greet(where):
        pl.semaphore_signal(barrier, inc=1, device_id=where, device_id_type=MESH)

    for k in range(1, nz):
        greet({"latent": same(k)})
    greet(across)
    greet(other_layer)
    greet(other_tok)
    for load in loads[1:] + we_loads:
        load.start()

    def remote(src, dst, ss, rs, where):
        return pltpu.make_async_remote_copy(
            src_ref=src, dst_ref=dst, send_sem=ss, recv_sem=rs,
            device_id=where, device_id_type=MESH,
        )

    lane = lax.broadcasted_iota(jnp.int32, (sub, LANES), 1) // rest

    def pack(full):
        out = jnp.zeros((sub, LANES), F32)
        for g in range(groups):
            out = jnp.where(lane == g, full[g * sub:(g + 1) * sub, main:], out)
        return jnp.concatenate(
            [full[:, i * LANES:(i + 1) * LANES] for i in range(tiles)] + [out], axis=0
        )

    def spread(block):
        packed = block[tiles * part:]
        zero = jnp.zeros_like(packed)
        parts = jnp.concatenate(
            [jnp.where(lane == g, packed, zero) for g in range(groups)], axis=0
        )
        return jnp.concatenate(
            [block[i * part:(i + 1) * part] for i in range(tiles)] + [parts], axis=1
        )

    def spread_all(ref, j):
        return [spread(ref[c, j]) for c in range(CHUNKS)]

    def gather(buf, ss, rs):
        def send(way, c, j):
            where = across if way == 0 else {"latent": same(way)}
            return remote(buf.at[c, j], buf.at[c, j], ss.at[way, c, j], rs.at[c, j], where)

        def own(c):
            send(0, c, lat).start()
            send(1, c, lat).start()
            pl.when(inner)(lambda: send(3, c, lat).start())
            send(2, c, lat).start()

        def relay(c, k):
            j = same(k)
            send(0, c, j).wait_recv()
            send(0, c, j).start()
            if k == 2:
                pl.when(inner)(lambda: send(1, c, j).start())

        def arrive(c, k):
            send(0, c, cross(k)).wait_recv()

        def finish():
            for c in range(CHUNKS):
                for k in range(nz):
                    send(0, c, same(k)).wait_send()
                send(1, c, lat).wait_send()
                send(2, c, lat).wait_send()

                @pl.when(inner)
                def _():
                    send(3, c, lat).wait_send()
                    send(1, c, same(2)).wait_send()

        return own, relay, arrive, finish

    x_own, x_relay, x_arrive, x_finish = gather(xb, x_ss, x_rs)
    g_own, g_relay, g_arrive, g_finish = gather(gb, g_ss, g_rs)

    def x_tok(i):
        return remote(
            xb.at[:, half * tok_o + i], xo.at[:, i], xo_ss.at[i], xo_rs.at[i], other_tok
        )

    def g_tok(c):
        return remote(gb.at[c], go.at[c], go_ss.at[c], go_rs.at[c], other_tok)

    def one(i, src, dst, c, where):
        return remote(src.at[c], dst.at[c], one_ss.at[i, c], one_rs.at[i, c], where)

    def y_copy(c):
        return one(0, ys, yr, c, other_layer)

    def a_copy(c):
        return one(1, act, act_o, c, other_tok)

    def h_copy(c):
        return one(2, hs, hr, c, other_layer)

    def p_copy(c):
        return one(3, gp, gp_o, c, other_tok)

    def x_send(c, k):
        return remote(xs.at[c, k], xr.at[c, k], xs_ss.at[c, k], xr_rs.at[c, k], across)

    def z_send(c, k):
        return remote(
            zs.at[c, k], cr.at[c, k], zs_ss.at[c, k], cr_rs.at[c, k], {"latent": same(k)}
        )

    def encode(c, j):
        pre[c] += jnp.dot(spread(xb[c, j]), we[j], preferred_element_type=F32)

    def y_out(c):
        ys[c] = pre[c].astype(BF16)
        y_copy(c).start()

    def activate(c):
        y_copy(c).wait_recv()
        v = BETA * (pre[c] + yr[c].astype(F32) + be_ref[...])
        e = jnp.exp(-jnp.abs(v))
        act[c] = ((jnp.maximum(v, 0.0) + jnp.log1p(e)) / BETA).astype(BF16)
        slope[c] = jnp.where(v >= 0, 1.0, e) / (1.0 + e)
        a_copy(c).start()

    def decode(c, j):
        return pack(jnp.dot(act[c], wd[j], preferred_element_type=F32))

    def x_out(c, k):
        xs[c, k] = decode(c, cross(k)).astype(BF16)
        x_send(c, k).start()

    def z_out(c, k):
        mine = decode(c, same(k))
        x_send(c, k).wait_recv()
        zs[c, k] = (mine + xr[c, k].astype(F32)).astype(BF16)
        z_send(c, k).start()

    def settle(c):
        total = decode(c, lat) + bias_x[c]
        x_send(c, 0).wait_recv()
        total += xr[c, 0].astype(F32)
        for k in range(1, nz):
            z_send(c, k).wait_recv()
            total += cr[c, k].astype(F32)
        gb[c, lat] = (2.0 / tokens * total).astype(BF16)
        g_own(c)

    def back(c, j):
        d = lax.dot_general(
            spread(gb[c, j]), wd[j], (((1,), (1,)), ((), ())), preferred_element_type=F32
        )
        pre[c] += d

    def back_first(c):
        pre[c] = lax.dot_general(
            spread(gb[c, lat]), wd[lat], (((1,), (1,)), ((), ())), preferred_element_type=F32
        )

    def h_out(c):
        hs[c] = pre[c].astype(BF16)
        h_copy(c).start()
        g_tok(c).start()

    def grad_pre(c):
        h_copy(c).wait_recv()
        gp[c] = ((pre[c] + hr[c].astype(F32)) * slope[c]).astype(BF16)
        p_copy(c).start()

    def both(own, other, j_own, j_other):
        return jnp.concatenate(spread_all(own, j_own) + spread_all(other, j_other), axis=0)

    def turn_x():
        for i in range(half):
            x_tok(i).wait_recv()
            xt[i] = both(xb, xo, half * tok + i, i).T

    def turn_act():
        for c in range(CHUNKS):
            a_copy(c).wait_recv()
        act_t[...] = jnp.concatenate(
            [act[c] for c in range(CHUNKS)] + [act_o[c] for c in range(CHUNKS)], axis=0
        ).T

    def widen_decoder():
        wd_load.wait()
        for k in range(n_lat):
            lo = k * feats
            w_rest = wdv[:, lo + main:lo + feats]
            wd[k] = jnp.concatenate([wdv[:, lo:lo + main]] + [w_rest] * groups, axis=1)

    def fill_bias():
        bias = bd_ref[...].astype(F32)
        bias = jnp.concatenate([bias[:, :main]] + [bias[:, main:]] * groups, axis=1)
        block = jnp.concatenate(
            [jnp.broadcast_to(bias[:, i * LANES:(i + 1) * LANES], (part, LANES)) for i in range(tiles)]
            + [jnp.broadcast_to(bias[:, main:], (sub, LANES))],
            axis=0,
        )
        for c in range(CHUNKS):
            bias_x[c] = block - xb[c, lat].astype(F32)

    x_load.wait()
    tail = x_ref[:, main:]
    wide = jnp.concatenate([x_ref[:, :main]] + [tail] * groups, axis=1).astype(F32)
    for c in range(CHUNKS):
        xb[c, lat] = pack(wide[c * part:(c + 1) * part]).astype(BF16)

    pl.semaphore_wait(barrier, nz + 2)
    for c in range(CHUNKS):
        x_own(c)
    for load in we_loads:
        load.wait()
    be_load.wait()
    bd_load.wait()
    for c in range(CHUNKS):
        pre[c] = jnp.dot(spread(xb[c, lat]), we[lat], preferred_element_type=F32)
    widen_decoder()
    fill_bias()

    def relay_encode(c):
        for k in range(1, nz):
            x_relay(c, k)
        for k in range(1, nz):
            encode(c, same(k))

    def arrive_encode(c):
        for k in range(nz):
            x_arrive(c, k)
            encode(c, cross(k))

    relay_encode(0)
    relay_encode(1)
    arrive_encode(0)
    y_out(0)
    relay_encode(2)
    arrive_encode(1)
    y_out(1)
    activate(0)
    for k in (3, 2, 1, 0):
        x_out(0, k)
    arrive_encode(2)
    y_out(2)
    for i in range(half):
        x_tok(i).start()
    activate(1)
    for k in (3, 2, 1, 0):
        x_out(1, k)
    for k in (3, 2, 1):
        z_out(0, k)
    activate(2)
    for k in (3, 2, 1, 0):
        x_out(2, k)
    for k in (3, 2, 1):
        z_out(1, k)
    turn_x()
    settle(0)
    for k in (3, 2, 1):
        z_out(2, k)
    turn_act()
    settle(1)
    back_first(0)

    def relay_back(c):
        for k in range(1, nz):
            g_relay(c, k)
        for k in range(1, nz):
            back(c, same(k))

    def arrive_back(c):
        for k in range(nz):
            g_arrive(c, k)
            back(c, cross(k))

    relay_back(0)
    settle(2)
    back_first(1)
    back_first(2)
    relay_back(1)
    arrive_back(0)
    h_out(0)
    relay_back(2)
    arrive_back(1)
    h_out(1)
    grad_pre(0)
    arrive_back(2)
    h_out(2)
    grad_pre(1)
    for c in range(CHUNKS):
        g_tok(c).wait_recv()

    row = []
    for j in range(n_lat):
        dw = jnp.dot(act_t[...], both(gb, go, j, j), preferred_element_type=F32)
        r = dw[:, main:main + rest]
        for g in range(1, groups):
            r = r + dw[:, main + g * rest:main + (g + 1) * rest]
        row += [dw[:, :main], r]
        if (j + 1) * feats % LANES == 0:
            width = sum(p.shape[1] for p in row)
            od_ref[:, (j + 1) * feats - width:(j + 1) * feats] = jnp.concatenate(
                row, axis=1
            ).astype(BF16)
            row = []

    grad_pre(2)
    for c in range(CHUNKS):
        p_copy(c).wait_recv()
    half_rows = CHUNKS * part
    for c in range(CHUNKS):
        gp_both[c * part:(c + 1) * part] = gp[c]
        gp_both[half_rows + c * part:half_rows + (c + 1) * part] = gp_o[c]

    x_finish()
    g_finish()
    for i in range(half):
        x_tok(i).wait_send()
    for c in range(CHUNKS):
        for copy in (g_tok, y_copy, a_copy, h_copy, p_copy):
            copy(c).wait_send()
        x_send(c, 0).wait_send()
        for k in range(1, nz):
            x_send(c, k).wait_send()
            z_send(c, k).wait_send()


def finish_kernel(gp_ref, xt_ref, dec_ref, oe_hbm, od_hbm, oe, sem, dec_sem):
    half, wide, _ = xt_ref.shape
    main = wide - LANES
    feats = oe.shape[1]
    rest = feats - main
    dec = pltpu.make_async_copy(dec_ref, od_hbm, dec_sem)
    dec.start()
    copies = []
    for i in range(half):
        dw = jnp.dot(xt_ref[i], gp_ref[...], preferred_element_type=F32)
        r = dw[main:main + rest]
        for g in range(1, LANES // rest):
            r = r + dw[main + g * rest:main + (g + 1) * rest]
        oe[i] = jnp.concatenate([dw[:main], r], axis=0).astype(BF16)
        copy = pltpu.make_async_copy(oe.at[i], oe_hbm.at[pl.ds(i * feats, feats)], sem.at[i])
        copy.start()
        copies.append(copy)
    for copy in copies:
        copy.wait()
    dec.wait()


def fused_shards(n_lat, resid, w_enc, b_enc, w_dec, b_dec):
    x, we, wd = resid[0], w_enc[0], w_dec[0]
    rows, feats = x.shape
    total, hid = we.shape
    main = feats // LANES * LANES
    wide = main + LANES
    groups = LANES // (feats - main)
    part = rows // CHUNKS
    block = part * feats // LANES
    half, nz = n_lat // 2, n_lat // 2
    dma = pltpu.SemaphoreType.DMA
    vm = pltpu.VMEM
    blocks = vm((CHUNKS, n_lat, block, LANES), BF16)
    blocks_z = vm((CHUNKS, nz, block, LANES), BF16)
    square = vm((CHUNKS, part, hid), BF16)
    square_f = vm((CHUNKS, part, hid), F32)
    in_vmem = pl.BlockSpec(memory_space=pltpu.VMEM)
    in_hbm = pl.BlockSpec(memory_space=pltpu.HBM)
    gp_both, xt, dec = pl.pallas_call(
        functools.partial(kernel, n_lat, rows * 2),
        out_shape=(
            jax.ShapeDtypeStruct((2 * rows, hid), BF16),
            jax.ShapeDtypeStruct((half, wide, 2 * rows), BF16),
            jax.ShapeDtypeStruct((hid, total), BF16),
        ),
        in_specs=[in_hbm] * 5,
        out_specs=(in_vmem,) * 3,
        scratch_shapes=[
            vm((rows, feats), BF16), vm((1, hid), F32), vm((1, feats), BF16),
            vm((n_lat, wide, hid), BF16),
            vm((hid, total), BF16),
            vm((n_lat, hid, wide), BF16),
            blocks,
            vm((CHUNKS, half, block, LANES), BF16),
            blocks, blocks,
            square_f, square_f,
            square, vm((hid, 2 * rows), BF16), square,
            square, square, square, square, square, square,
            blocks_z, blocks_z, blocks_z, blocks_z,
            vm((CHUNKS, block, LANES), F32),
            dma((4,)), dma((n_lat, 1 + groups)),
            dma((4, CHUNKS, n_lat)), dma((CHUNKS, n_lat)), dma((half,)), dma((half,)),
            dma((4, CHUNKS, n_lat)), dma((CHUNKS, n_lat)), dma((CHUNKS,)), dma((CHUNKS,)),
            dma((4, CHUNKS)), dma((4, CHUNKS)),
            dma((CHUNKS, nz)), dma((CHUNKS, nz)), dma((CHUNKS, nz)), dma((CHUNKS, nz)),
        ],
        compiler_params=pltpu.CompilerParams(
            collective_id=0, has_side_effects=True, vmem_limit_bytes=48 * 2**20
        ),
    )(*(
        pltpu.with_memory_space_constraint(v, pltpu.HBM)
        for v in (x, we, b_enc.reshape(1, -1), wd, b_dec)
    ))
    ge, gd = pl.pallas_call(
        finish_kernel,
        out_shape=(
            jax.ShapeDtypeStruct((half * feats, hid), BF16),
            jax.ShapeDtypeStruct((hid, total), BF16),
        ),
        in_specs=[in_vmem] * 3,
        out_specs=(in_hbm, in_hbm),
        scratch_shapes=[vm((half, feats, hid), BF16), dma((half,)), dma(())],
        compiler_params=pltpu.CompilerParams(vmem_limit_bytes=8 * 2**20),
    )(gp_both, xt, dec)
    return ge[None], gd[None]


def packs(mesh, rows, feats):
    rest = feats % LANES
    if mesh.shape["layer"] != 2 or mesh.shape["tok"] != 2 or mesh.shape["latent"] != 8:
        return False
    if rest == 0 or rest % 32 or LANES % rest:
        return False
    return rows % (16 * CHUNKS * (LANES // rest)) == 0 and feats > LANES


def solution(mesh):
    def shards(resid, w_enc, b_enc, w_dec, b_dec):
        _, rows, feats = resid.shape
        if packs(mesh, rows, feats) and resid.shape[0] == 1:
            return fused_shards(mesh.shape["latent"], resid, w_enc, b_enc, w_dec, b_dec)
        return plain_shards(resid, w_enc, b_enc, w_dec, b_dec)

    placed = (
        P("layer", "tok", "latent"),
        P("layer", None, "latent"),
        P("latent"),
        P("layer", "latent", None),
        P("layer", "latent"),
    )
    return jax.shard_map(
        shards,
        mesh=mesh,
        in_specs=placed,
        out_specs=(P("layer", "tok", "latent"), P("layer", "latent", None)),
        check_vma=False,
    )
```

```python
import functools

import jax
import jax.numpy as jnp
from jax import lax
from jax.experimental import pallas as pl
from jax.experimental.pallas import tpu as pltpu
from jax.sharding import PartitionSpec as P

BETA = 4.0
LANES = 128
CHUNKS = 3
MESH = pl.DeviceIdType.MESH
F32 = jnp.float32
BF16 = jnp.bfloat16


def plain_shards(resid, w_enc, b_enc, w_dec, b_dec):
    decoder = w_dec[0]
    x_full = lax.all_gather(resid, "latent", axis=2, tiled=True)[0]
    bias_full = lax.all_gather(b_dec.reshape(1, 1, -1), "latent", axis=2, tiled=True)
    bias_full = bias_full.reshape(-1).astype(F32)
    tokens = x_full.shape[0] * lax.axis_size("tok")
    partial_value = jnp.dot(x_full, w_enc[0], preferred_element_type=F32)
    pre = lax.psum(partial_value.astype(BF16), "layer").astype(F32) + b_enc
    act = (jax.nn.softplus(BETA * pre) / BETA).astype(BF16)
    slope = jax.nn.sigmoid(BETA * pre)
    recon = lax.psum(
        jnp.dot(act, decoder, preferred_element_type=F32).astype(BF16), "latent"
    ).astype(F32)
    grad_all = (2.0 / tokens * (recon + bias_full - x_full.astype(F32))).astype(BF16)
    dec_sum = lax.dot_general(
        act, grad_all, (((0,), (0,)), ((), ())), preferred_element_type=F32
    )
    act_grad = lax.dot_general(
        grad_all, decoder, (((1,), (1,)), ((), ())), preferred_element_type=F32
    )
    grad_act = lax.psum(act_grad.astype(BF16), "layer").astype(F32)
    grad_pre = (grad_act * slope).astype(BF16)
    grad_w_dec = lax.psum(dec_sum.astype(BF16), "tok")
    grad_w_enc = lax.psum_scatter(
        lax.dot_general(
            x_full, grad_pre, (((0,), (0,)), ((), ())), preferred_element_type=F32
        ).astype(BF16),
        "tok",
        scatter_dimension=0,
        tiled=True,
    )
    return (grad_w_enc[None], grad_w_dec[None])


def kernel(
    n_lat, tokens,
    x_hbm, we_hbm, be_hbm, wd_hbm, bd_hbm,
    gp_both, xt, od_ref,
    x_ref, be_ref, bd_ref, we, wdv, wd, xb, xo, gb, go, pre, slope, act, act_t, act_o, ys, yr, hs, hr, gp, gp_o,
    xs, xr, zs, cr, bias_x,
    load_sem, we_sem, x_ss, x_rs, xo_ss, xo_rs, g_ss, g_rs, go_ss, go_rs, one_ss, one_rs, xs_ss, xr_rs, zs_ss, cr_rs,
):
    rows, feats = x_ref.shape
    hid = we.shape[2]
    main = feats // LANES * LANES
    tiles = main // LANES
    rest = feats - main
    groups = LANES // rest
    part = rows // CHUNKS
    sub = part // groups
    nz = n_lat // 2
    half = n_lat // 2

    lay = lax.axis_index("layer")
    lat = lax.axis_index("latent")
    tok = lax.axis_index("tok")
    z, xx = lat // 2, lat % 2
    across = {"latent": 2 * z + 1 - xx}
    other_layer = {"layer": 1 - lay}
    tok_o = 1 - tok
    other_tok = {"tok": tok_o}
    inner = jnp.logical_and(z > 0, z < nz - 1)

    def peer(k):
        if k == 0:
            return z
        if k == 1:
            return z + 1 - 2 * (z % 2)
        if k == 2:
            return (z + 2) % 4
        return nz - 1 - z

    def same(k):
        return 2 * peer(k) + xx

    def cross(k):
        return 2 * peer(k) + 1 - xx

    def slot(zt, side):
        return peer(zt) + nz * ((side + xx) % 2)

    def tok_slot(of, i):
        low, high = slot(i // 2, i % 2), slot(nz // 2 + i // 2, i % 2)
        return jnp.where(of == 0, low, high)

    loads = [
        pltpu.make_async_copy(src, dst, load_sem.at[i])
        for i, (src, dst) in enumerate(
            [(x_hbm, x_ref), (wd_hbm, wdv), (be_hbm, be_ref), (bd_hbm, bd_ref)]
        )
    ]
    we_loads = []
    for j in range(n_lat):
        lo = (same(j) if j < nz else cross(j - nz)) * feats
        lo, after = pl.multiple_of(lo, rest), pl.multiple_of(lo + main, rest)
        we_loads.append(pltpu.make_async_copy(
            we_hbm.at[pl.ds(lo, main)], we.at[j, pl.ds(0, main)], we_sem.at[j, 0]
        ))
        for g in range(groups):
            we_loads.append(pltpu.make_async_copy(
                we_hbm.at[pl.ds(after, rest)], we.at[j, pl.ds(main + g * rest, rest)],
                we_sem.at[j, 1 + g],
            ))
    loads[0].start()
    x_load, wd_load, be_load, bd_load = loads

    barrier = pltpu.get_barrier_semaphore()

    def greet(where):
        pl.semaphore_signal(barrier, inc=1, device_id=where, device_id_type=MESH)

    for k in range(1, nz):
        greet({"latent": same(k)})
    greet(across)
    greet(other_layer)
    greet(other_tok)
    for load in loads[1:] + we_loads:
        load.start()

    def remote(src, dst, ss, rs, where):
        return pltpu.make_async_remote_copy(
            src_ref=src, dst_ref=dst, send_sem=ss, recv_sem=rs,
            device_id=where, device_id_type=MESH,
        )

    lane = lax.broadcasted_iota(jnp.int32, (sub, LANES), 1) // rest

    def pack(full):
        out = jnp.zeros((sub, LANES), F32)
        for g in range(groups):
            out = jnp.where(lane == g, full[g * sub:(g + 1) * sub, main:], out)
        return jnp.concatenate(
            [full[:, i * LANES:(i + 1) * LANES] for i in range(tiles)] + [out], axis=0
        )

    def spread(block):
        packed = block[tiles * part:]
        zero = jnp.zeros_like(packed)
        parts = jnp.concatenate(
            [jnp.where(lane == g, packed, zero) for g in range(groups)], axis=0
        )
        return jnp.concatenate(
            [block[i * part:(i + 1) * part] for i in range(tiles)] + [parts], axis=1
        )

    def spread_all(ref, j):
        return [spread(ref[c, j]) for c in range(CHUNKS)]

    def gather(buf, ss, rs):
        def send(way, c, j, to):
            where = across if way == 0 else {"latent": same(way)}
            return remote(buf.at[c, j], buf.at[c, to], ss.at[way, c, j], rs.at[c, to], where)

        def own(c):
            send(0, c, 0, nz).start()
            send(2, c, 0, 2).start()
            send(1, c, 0, 1).start()
            pl.when(inner)(lambda: send(3, c, 0, 3).start())

        def relay(c, k):
            send(k, c, 0, k).wait_recv()
            send(0, c, k, nz + k).start()
            if k == 2:
                pl.when(inner)(lambda: send(1, c, 2, 3).start())

        def arrive(c, k):
            send(0, c, k, nz + k).wait_recv()

        def finish():
            for c in range(CHUNKS):
                for k in range(nz):
                    send(0, c, k, nz + k).wait_send()
                send(1, c, 0, 1).wait_send()
                send(2, c, 0, 2).wait_send()

                @pl.when(inner)
                def _():
                    send(3, c, 0, 3).wait_send()
                    send(1, c, 2, 3).wait_send()

        return own, relay, arrive, finish

    x_own, x_relay, x_arrive, x_finish = gather(xb, x_ss, x_rs)
    g_own, g_relay, g_arrive, g_finish = gather(gb, g_ss, g_rs)

    def x_tok(i):
        return remote(
            xb.at[:, tok_slot(tok_o, i)], xo.at[:, i], xo_ss.at[i], xo_rs.at[i], other_tok
        )

    def g_tok(c):
        return remote(gb.at[c], go.at[c], go_ss.at[c], go_rs.at[c], other_tok)

    def one(i, src, dst, c, where):
        return remote(src.at[c], dst.at[c], one_ss.at[i, c], one_rs.at[i, c], where)

    def y_copy(c):
        return one(0, ys, yr, c, other_layer)

    def a_copy(c):
        return one(1, act, act_o, c, other_tok)

    def h_copy(c):
        return one(2, hs, hr, c, other_layer)

    def p_copy(c):
        return one(3, gp, gp_o, c, other_tok)

    def x_send(c, k):
        return remote(xs.at[c, k], xr.at[c, k], xs_ss.at[c, k], xr_rs.at[c, k], across)

    def z_send(c, k):
        return remote(
            zs.at[c, k], cr.at[c, k], zs_ss.at[c, k], cr_rs.at[c, k], {"latent": same(k)}
        )

    def encode(c, j):
        pre[c] += jnp.dot(spread(xb[c, j]), we[j], preferred_element_type=F32)

    def y_out(c):
        ys[c] = pre[c].astype(BF16)
        y_copy(c).start()

    def activate(c):
        y_copy(c).wait_recv()
        v = BETA * (pre[c] + yr[c].astype(F32) + be_ref[...])
        e = jnp.exp(-jnp.abs(v))
        act[c] = ((jnp.maximum(v, 0.0) + jnp.log1p(e)) / BETA).astype(BF16)
        slope[c] = jnp.where(v >= 0, 1.0, e) / (1.0 + e)
        a_copy(c).start()

    def decode(c, j):
        return pack(jnp.dot(act[c], wd[j], preferred_element_type=F32))

    def x_out(c, k):
        xs[c, k] = decode(c, nz + k).astype(BF16)
        x_send(c, k).start()

    def z_out(c, k):
        mine = decode(c, k)
        x_send(c, k).wait_recv()
        zs[c, k] = (mine + xr[c, k].astype(F32)).astype(BF16)
        z_send(c, k).start()

    def settle(c):
        total = decode(c, 0) + bias_x[c]
        x_send(c, 0).wait_recv()
        total += xr[c, 0].astype(F32)
        for k in range(1, nz):
            z_send(c, k).wait_recv()
            total += cr[c, k].astype(F32)
        gb[c, 0] = (2.0 / tokens * total).astype(BF16)
        g_own(c)

    def back(c, j):
        d = lax.dot_general(
            spread(gb[c, j]), wd[j], (((1,), (1,)), ((), ())), preferred_element_type=F32
        )
        pre[c] += d

    def back_first(c):
        pre[c] = lax.dot_general(
            spread(gb[c, 0]), wd[0], (((1,), (1,)), ((), ())), preferred_element_type=F32
        )

    def h_out(c):
        hs[c] = pre[c].astype(BF16)
        h_copy(c).start()
        g_tok(c).start()

    def grad_pre(c):
        h_copy(c).wait_recv()
        value = ((pre[c] + hr[c].astype(F32)) * slope[c]).astype(BF16)
        gp[c] = value
        p_copy(c).start()
        gp_both[c * part:(c + 1) * part] = value

    def both(own, other, j_own, j_other):
        return jnp.concatenate(spread_all(own, j_own) + spread_all(other, j_other), axis=0)

    def turn_x():
        for i in range(half):
            x_tok(i).wait_recv()
            xt[i] = both(xb, xo, tok_slot(tok, i), i).T

    def turn_act():
        for c in range(CHUNKS):
            a_copy(c).wait_recv()
        act_t[...] = jnp.concatenate(
            [act[c] for c in range(CHUNKS)] + [act_o[c] for c in range(CHUNKS)], axis=0
        ).T

    def widen_decoder():
        wd_load.wait()
        for k in range(n_lat):
            lo = k * feats
            w_rest = wdv[:, lo + main:lo + feats]
            wd[slot(k // 2, k % 2)] = jnp.concatenate([wdv[:, lo:lo + main]] + [w_rest] * groups, axis=1)

    def fill_bias():
        bias = bd_ref[...].astype(F32)
        bias = jnp.concatenate([bias[:, :main]] + [bias[:, main:]] * groups, axis=1)
        block = jnp.concatenate(
            [jnp.broadcast_to(bias[:, i * LANES:(i + 1) * LANES], (part, LANES)) for i in range(tiles)]
            + [jnp.broadcast_to(bias[:, main:], (sub, LANES))],
            axis=0,
        )
        for c in range(CHUNKS):
            bias_x[c] = block - xb[c, 0].astype(F32)

    def other_pre(c):
        gp_both[rows + c * part:rows + (c + 1) * part] = gp_o[c]

    def dec_grad(first, last):
        row = []
        for j in range(first, last):
            at = slot(j // 2, j % 2)
            dw = jnp.dot(act_t[...], both(gb, go, at, at), preferred_element_type=F32)
            r = dw[:, main:main + rest]
            for g in range(1, groups):
                r = r + dw[:, main + g * rest:main + (g + 1) * rest]
            row += [dw[:, :main], r]
            if (j + 1) * feats % LANES == 0:
                width = sum(p.shape[1] for p in row)
                od_ref[:, (j + 1) * feats - width:(j + 1) * feats] = jnp.concatenate(
                    row, axis=1
                ).astype(BF16)
                row = []

    def sums_finish():
        for c in range(CHUNKS):
            for copy in (y_copy, a_copy):
                copy(c).wait_send()
            x_send(c, 0).wait_send()
            for k in range(1, nz):
                x_send(c, k).wait_send()
                z_send(c, k).wait_send()

    x_load.wait()
    tail = x_ref[:, main:]
    wide = jnp.concatenate([x_ref[:, :main]] + [tail] * groups, axis=1).astype(F32)
    for c in range(CHUNKS):
        xb[c, 0] = pack(wide[c * part:(c + 1) * part]).astype(BF16)

    pl.semaphore_wait(barrier, nz + 2)
    for c in range(CHUNKS):
        x_own(c)
    for load in we_loads:
        load.wait()
    be_load.wait()
    bd_load.wait()
    for c in range(CHUNKS):
        pre[c] = jnp.dot(spread(xb[c, 0]), we[0], preferred_element_type=F32)
    widen_decoder()
    fill_bias()

    def relay_encode(c):
        for k in range(1, nz):
            x_relay(c, k)
        for k in range(1, nz):
            encode(c, k)

    def arrive_encode(c):
        for k in range(nz):
            x_arrive(c, k)
            encode(c, nz + k)

    relay_encode(0)
    relay_encode(1)
    arrive_encode(0)
    y_out(0)
    relay_encode(2)
    arrive_encode(1)
    y_out(1)
    activate(0)
    for k in (3, 2, 1, 0):
        x_out(0, k)
    arrive_encode(2)
    y_out(2)
    for i in range(half):
        x_tok(i).start()
    activate(1)
    for k in (3, 2, 1, 0):
        x_out(1, k)
    for k in (3, 2, 1):
        z_out(0, k)
    activate(2)
    for k in (3, 2, 1, 0):
        x_out(2, k)
    for k in (3, 2, 1):
        z_out(1, k)
    turn_x()
    settle(0)
    for k in (3, 2, 1):
        z_out(2, k)
    turn_act()
    x_finish()
    for i in range(half):
        x_tok(i).wait_send()
    settle(1)
    back_first(0)

    def relay_back(c):
        for k in range(1, nz):
            g_relay(c, k)
        for k in range(1, nz):
            back(c, k)

    def arrive_back(c):
        for k in range(nz):
            g_arrive(c, k)
            back(c, nz + k)

    relay_back(0)
    settle(2)
    back_first(1)
    back_first(2)
    relay_back(1)
    arrive_back(0)
    h_out(0)
    relay_back(2)
    arrive_back(1)
    h_out(1)
    grad_pre(0)
    sums_finish()
    arrive_back(2)
    h_out(2)
    grad_pre(1)
    p_copy(0).wait_recv()
    other_pre(0)
    for c in range(CHUNKS):
        g_tok(c).wait_recv()
    dec_grad(0, half)
    grad_pre(2)
    g_finish()
    dec_grad(half, n_lat)
    for c in range(CHUNKS):
        for copy in (g_tok, h_copy, p_copy):
            copy(c).wait_send()
    for c in range(1, CHUNKS):
        p_copy(c).wait_recv()
        other_pre(c)


def finish_kernel(gp_ref, xt_ref, dec_ref, oe_hbm, od_hbm, oe, sem, dec_sem):
    half, wide, _ = xt_ref.shape
    main = wide - LANES
    feats = oe.shape[1]
    rest = feats - main
    dec = pltpu.make_async_copy(dec_ref, od_hbm, dec_sem)
    dec.start()
    copies = []
    for i in range(half):
        dw = jnp.dot(xt_ref[i], gp_ref[...], preferred_element_type=F32)
        r = dw[main:main + rest]
        for g in range(1, LANES // rest):
            r = r + dw[main + g * rest:main + (g + 1) * rest]
        oe[i] = jnp.concatenate([dw[:main], r], axis=0).astype(BF16)
        copy = pltpu.make_async_copy(oe.at[i], oe_hbm.at[pl.ds(i * feats, feats)], sem.at[i])
        copy.start()
        copies.append(copy)
    for copy in copies:
        copy.wait()
    dec.wait()


def fused_shards(n_lat, resid, w_enc, b_enc, w_dec, b_dec):
    x, we, wd = resid[0], w_enc[0], w_dec[0]
    rows, feats = x.shape
    total, hid = we.shape
    main = feats // LANES * LANES
    wide = main + LANES
    groups = LANES // (feats - main)
    part = rows // CHUNKS
    block = part * feats // LANES
    half, nz = n_lat // 2, n_lat // 2
    dma = pltpu.SemaphoreType.DMA
    vm = pltpu.VMEM
    blocks = vm((CHUNKS, n_lat, block, LANES), BF16)
    blocks_z = vm((CHUNKS, nz, block, LANES), BF16)
    square = vm((CHUNKS, part, hid), BF16)
    square_f = vm((CHUNKS, part, hid), F32)
    in_vmem = pl.BlockSpec(memory_space=pltpu.VMEM)
    in_hbm = pl.BlockSpec(memory_space=pltpu.HBM)
    gp_both, xt, dec = pl.pallas_call(
        functools.partial(kernel, n_lat, rows * 2),
        out_shape=(
            jax.ShapeDtypeStruct((2 * rows, hid), BF16),
            jax.ShapeDtypeStruct((half, wide, 2 * rows), BF16),
            jax.ShapeDtypeStruct((hid, total), BF16),
        ),
        in_specs=[in_hbm] * 5,
        out_specs=(in_vmem,) * 3,
        scratch_shapes=[
            vm((rows, feats), BF16), vm((1, hid), F32), vm((1, feats), BF16),
            vm((n_lat, wide, hid), BF16),
            vm((hid, total), BF16),
            vm((n_lat, hid, wide), BF16),
            blocks,
            vm((CHUNKS, half, block, LANES), BF16),
            blocks, blocks,
            square_f, square_f,
            square, vm((hid, 2 * rows), BF16), square,
            square, square, square, square, square, square,
            blocks_z, blocks_z, blocks_z, blocks_z,
            vm((CHUNKS, block, LANES), F32),
            dma((4,)), dma((n_lat, 1 + groups)),
            dma((4, CHUNKS, n_lat)), dma((CHUNKS, n_lat)), dma((half,)), dma((half,)),
            dma((4, CHUNKS, n_lat)), dma((CHUNKS, n_lat)), dma((CHUNKS,)), dma((CHUNKS,)),
            dma((4, CHUNKS)), dma((4, CHUNKS)),
            dma((CHUNKS, nz)), dma((CHUNKS, nz)), dma((CHUNKS, nz)), dma((CHUNKS, nz)),
        ],
        compiler_params=pltpu.CompilerParams(
            collective_id=0, has_side_effects=True, vmem_limit_bytes=48 * 2**20
        ),
    )(*(
        pltpu.with_memory_space_constraint(v, pltpu.HBM)
        for v in (x, we, b_enc.reshape(1, -1), wd, b_dec)
    ))
    ge, gd = pl.pallas_call(
        finish_kernel,
        out_shape=(
            jax.ShapeDtypeStruct((half * feats, hid), BF16),
            jax.ShapeDtypeStruct((hid, total), BF16),
        ),
        in_specs=[in_vmem] * 3,
        out_specs=(in_hbm, in_hbm),
        scratch_shapes=[vm((half, feats, hid), BF16), dma((half,)), dma(())],
        compiler_params=pltpu.CompilerParams(vmem_limit_bytes=8 * 2**20),
    )(gp_both, xt, dec)
    return ge[None], gd[None]


def packs(mesh, rows, feats):
    rest = feats % LANES
    if mesh.shape["layer"] != 2 or mesh.shape["tok"] != 2 or mesh.shape["latent"] != 8:
        return False
    if rest == 0 or rest % 32 or LANES % rest:
        return False
    return rows % (16 * CHUNKS * (LANES // rest)) == 0 and feats > LANES


def solution(mesh):
    def shards(resid, w_enc, b_enc, w_dec, b_dec):
        _, rows, feats = resid.shape
        if packs(mesh, rows, feats) and resid.shape[0] == 1:
            return fused_shards(mesh.shape["latent"], resid, w_enc, b_enc, w_dec, b_dec)
        return plain_shards(resid, w_enc, b_enc, w_dec, b_dec)

    placed = (
        P("layer", "tok", "latent"),
        P("layer", None, "latent"),
        P("latent"),
        P("layer", "latent", None),
        P("layer", "latent"),
    )
    return jax.shard_map(
        shards,
        mesh=mesh,
        in_specs=placed,
        out_specs=(P("layer", "tok", "latent"), P("layer", "latent", None)),
        check_vma=False,
    )
```
